512 devices in a mesh: modes: 64 (over z_lo, x, core), rad: 8 (over z_hi, y).
Axes of the slice: x: 4, y: 4, z: 16 (z_hi: 2, z_lo: 8; z = z_hi * 8 + z_lo), core: 2. Of those that a mesh axis runs over, the one named last changes fastest.
Arguments:
- forcing: bfloat16 [3, 1024, 256, 256], P(None, 'modes', 'rad'), may hold values from -6 to 6
- diffusion: float32 [3], replicated, may hold values from 0.05 to 1
- axial_forward: float32 [256, 256], replicated, may hold values from -0.375 to 0.375
- axial_inverse_map: float32 [256, 256], replicated, may hold values from -0.375 to 0.375
- axial_eigenvalues: float32 [256], replicated, may hold values from 0.05 to 10
- radial_forward: float32 [512, 256, 256], P(('modes', 'rad')), may hold values from -0.375 to 0.375
- radial_backward: float32 [512, 256, 256], P(('modes', 'rad')), may hold values from -0.375 to 0.375
- radial_eigenvalues: float32 [512, 256], P(('modes', 'rad')), may hold values from 0.05 to 10
Outputs:
- solution: float32 [3, 512, 2, 256, 256], P(None, 'modes', None, 'rad')
The draws below stay inside these ranges and needn't reach their ends.
All inputs are finite; a program needn't handle non-finite values.
Results may differ from the reference program's by a relative error of at most 0.0003.
Values may be sent and summed in bfloat16 or wider, within the bound.
A program may use at most 64 MiB of HBM per device.

```python
import math
import jax
import jax.numpy as jnp
from jax import lax

FIELDS = 3
NT = 1024
NR = 256
NZ = 256
MODES = 512


def block_levels(stream_key, dims, split, smallest, high):
    gain, own = 1.0, jax.random.fold_in(stream_key, 6)
    for axis_at, shards_of in split:
        heights = jnp.exp(jax.random.uniform(jax.random.fold_in(own, axis_at), (shards_of,), jnp.float32, smallest / len(split), high / len(split)))
        gain = gain * jnp.repeat(heights, dims[axis_at] // shards_of).reshape([-1 if axis == axis_at else 1 for axis in range(len(dims))])
    return gain


def noise(stream_key, dims, width, bound, cuts=(), kind=jnp.bfloat16):
    gain = block_levels(stream_key, dims, cuts, -0.22, 0.18) if cuts else 1.0
    drawn = jax.random.normal(stream_key, dims, jnp.float32) * width * gain
    return jnp.minimum(jnp.maximum(drawn, -bound), bound).astype(kind)


def setup_inputs(seed: int = 0) -> dict:
    key_list = jax.random.split(jax.random.key(seed), 9)
    forcing = noise(key_list[0], (FIELDS, NT, NR, NZ), 1.0, 6.0, ((1, 64), (2, 8)))
    diffusion = jnp.clip(jnp.exp(jax.random.uniform(key_list[1], (FIELDS,), jnp.float32, math.log(0.05), math.log(1.0))), 0.05, 1.0)
    axial_forward = noise(key_list[2], (NZ, NZ), NZ ** -0.5, 0.375, (), jnp.float32)
    axial_inverse_map = noise(key_list[3], (NZ, NZ), NZ ** -0.5, 0.375, (), jnp.float32)
    axial_eigenvalues = jnp.clip(jnp.exp(jax.random.uniform(key_list[4], (NZ,), jnp.float32, math.log(0.05), math.log(10.0))), 0.05, 10.0)
    radial_forward = noise(key_list[5], (MODES, NR, NR), NR ** -0.5, 0.375, ((0, 512),), jnp.float32)
    radial_backward = noise(key_list[6], (MODES, NR, NR), NR ** -0.5, 0.375, ((0, 512),), jnp.float32)
    radial_eigenvalues = jnp.clip(jnp.exp(math.log(10.0) - 5.2983174 * jax.random.uniform(key_list[7], (MODES, NR), jnp.float32) ** block_levels(key_list[7], (MODES, NR), ((0, 512),), -0.2, 0.2)), 0.05, 10.0)
    return dict(forcing=forcing, diffusion=diffusion, axial_forward=axial_forward, axial_inverse_map=axial_inverse_map, axial_eigenvalues=axial_eigenvalues, radial_forward=radial_forward, radial_backward=radial_backward, radial_eigenvalues=radial_eigenvalues)


def azimuthal_part(field_values):
    spectrum = jnp.fft.rfft(field_values.astype(jnp.float32), axis=0)[:MODES] * (1.0 / math.sqrt(NT))
    return jnp.stack([jnp.real(spectrum), jnp.imag(spectrum)], axis=1)

def reference(forcing, diffusion, axial_forward, axial_inverse_map, axial_eigenvalues, radial_forward, radial_backward, radial_eigenvalues):
    spectrum = lax.map(azimuthal_part, forcing)
    by_mode = jnp.transpose(spectrum, (1, 0, 2, 3, 4))
    highest_mode = lax.Precision.HIGHEST

    def modal_solve(operands):
        spectral_coefficients, forward_map, backward, eigenvalues = operands
        axial_coef = jnp.einsum('fcrz,qz->fcrq', spectral_coefficients, axial_forward, precision=highest_mode)
        radial_coefficients = jnp.einsum('ir,fcrq->fciq', forward_map, axial_coef, precision=highest_mode)
        denominator = 1.0 + diffusion[:, None, None, None] * (eigenvalues[None, None, :, None] + axial_eigenvalues[None, None, None, :])
        scaled = radial_coefficients / denominator
        returned = jnp.einsum('ri,fciq->fcrq', backward, scaled, precision=highest_mode)
        return jnp.einsum('zq,fcrq->fcrz', axial_inverse_map, returned, precision=highest_mode)
    solved = lax.map(modal_solve, (by_mode, radial_forward, radial_backward, radial_eigenvalues))
    return jnp.transpose(solved, (1, 0, 2, 3, 4))
```

```python
import math

import jax
import jax.numpy as jnp
from jax import lax
from jax.sharding import PartitionSpec as P

GLOBAL = True


def split_table(points, rows):
    k = jnp.arange(rows, dtype=jnp.int32)
    t = jnp.arange(points, dtype=jnp.int32)
    quarter = (k % 2).astype(jnp.float32) * (0.5 * math.pi)
    phase = ((k // 2)[:, None] * t[None, :]) % points
    radians = phase.astype(jnp.float32) * (2.0 * math.pi / points) + quarter[:, None]
    table = jnp.cos(radians) * (1.0 / math.sqrt(points))
    upper = table.astype(jnp.bfloat16)
    widened = lax.optimization_barrier(upper).astype(jnp.float32)
    lower = (table - widened).astype(jnp.bfloat16)
    return upper, lower


def per_device(forcing, diffusion, axial_forward, axial_inverse_map, axial_eigenvalues,
               radial_forward, radial_backward, radial_eigenvalues):
    hi = lax.Precision.HIGHEST
    fields, slab, rblock, nz = forcing.shape
    nm, nrad = lax.axis_size("modes"), lax.axis_size("rad")
    points = slab * nm
    nr = rblock * nrad
    modes = nm * nrad
    cols = rblock * nz // nm
    halves = nz // cols
    up, lo = split_table(points, 2 * modes)
    x = forcing.reshape(fields, slab, rblock, halves, cols)
    x = x.transpose(2, 3, 0, 1, 4).reshape(nm, fields, slab, cols)
    got = lax.all_to_all(x, "modes", split_axis=0, concat_axis=0, tiled=True)
    got = got.transpose(0, 2, 1, 3).reshape(points, fields * cols)
    spec = jnp.dot(up, got, preferred_element_type=jnp.float32) + jnp.dot(
        lo, got, preferred_element_type=jnp.float32)
    if GLOBAL:
        spec = spec.reshape(modes, 2, fields * cols)
        here = lax.all_to_all(spec, ("modes", "rad"), split_axis=0, concat_axis=0, tiled=True)
        here = here.reshape(nm, nrad, 2, fields, cols)
    else:
        spec = spec.reshape(nm, nrad, 2, fields * cols)
        here = lax.all_to_all(spec, "modes", split_axis=0, concat_axis=0, tiled=True)
        here = lax.all_to_all(here, "rad", split_axis=1, concat_axis=1, tiled=True)
        here = here.reshape(nm, nrad, 2, fields, cols)
    here = here.reshape(rblock, halves, nrad, 2, fields, cols)
    here = here.transpose(4, 3, 2, 0, 1, 5).reshape(fields, 2, nr, nz)
    axial = jnp.einsum("fcrz,qz->fcrq", here, axial_forward, precision=hi)
    radial = jnp.einsum("ir,fcrq->fciq", radial_forward[0], axial, precision=hi)
    denominator = 1.0 + diffusion[:, None, None, None] * (
        radial_eigenvalues[0][None, None, :, None] + axial_eigenvalues[None, None, None, :])
    scaled = radial / denominator
    returned = jnp.einsum("ri,fciq->fcrq", radial_backward[0], scaled, precision=hi)
    out = jnp.einsum("zq,fcrq->fcrz", axial_inverse_map, returned, precision=hi)
    out = out.reshape(fields, 1, 2, nr, nz)
    return lax.all_to_all(out, "rad", split_axis=3, concat_axis=1, tiled=True)


def solution(mesh):
    in_specs = (P(None, "modes", "rad", None), P(), P(), P(), P(),
                P(("modes", "rad"), None, None), P(("modes", "rad"), None, None),
                P(("modes", "rad"), None))
    return jax.shard_map(per_device, mesh=mesh, in_specs=in_specs,
                         out_specs=P(None, "modes", None, "rad", None), check_vma=False)
```

```python
import functools
import math

import jax
import jax.numpy as jnp
from jax import lax
from jax.experimental import pallas as pl
from jax.experimental.pallas import tpu as pltpu
from jax.sharding import PartitionSpec as P

F32, BF16 = jnp.float32, jnp.bfloat16
SPECTRUM_OCTAVES, SOLVED_OCTAVES = 16, 10


def encode(x, inverse_floor, octaves):
    grown = jnp.log2(1.0 + jnp.abs(x) * inverse_floor)
    code = jnp.exp2(grown * (239.0 / octaves) - 120.0)
    return jnp.where(x < 0, -code, code).astype(BF16)


def decode(code, floor, octaves):
    code = code.astype(F32)
    grown = (jnp.log2(jnp.abs(code)) + 120.0) * (octaves / 239.0)
    size = (jnp.exp2(grown) - 1.0) * floor
    return jnp.where(code < 0, -size, size)


def split(x):
    high = x.astype(BF16)
    return high, (x - high.astype(F32)).astype(BF16)


def dot3(a, b, dims):
    d = functools.partial(lax.dot_general, dimension_numbers=(dims, ((), ())), preferred_element_type=F32)
    return d(a[0], b[0]) + (d(a[0], b[1]) + d(a[1], b[0]))


NN, NT_ = ((1,), (0,)), ((1,), (1,))


def azimuthal_tables(points, rows):
    step = 32
    t = jnp.arange(points, dtype=jnp.int32)
    turn = 2.0 * math.pi / points

    def angles(k):
        return ((k[:, None] * t[None, :]) % points).astype(F32) * turn

    coarse = angles(step * jnp.arange(rows // 2 // step, dtype=jnp.int32))
    fine = angles(jnp.arange(step, dtype=jnp.int32))
    scale = 1.0 / math.sqrt(points)
    ca, sa, cb, sb = lax.optimization_barrier(
        (jnp.cos(coarse), jnp.sin(coarse), jnp.cos(fine) * scale, jnp.sin(fine) * scale))
    ca, sa = ca[:, None], sa[:, None]
    real = ca * cb[None] - sa * sb[None]
    imag = -(sa * cb[None] + ca * sb[None])
    table = jnp.stack([real, imag], axis=2).reshape(rows, points)
    upper = table.astype(BF16)
    lower = (table - lax.optimization_barrier(upper).astype(F32)).astype(BF16)
    return upper, lower


def transform_kernel(up_ref, lo_ref, got_ref, bound_ref, out_ref):
    fields = got_ref.shape[1]
    points, cols = got_ref.shape[0] * got_ref.shape[2], got_ref.shape[3]
    inverse_floor = 2.0 ** (SPECTRUM_OCTAVES - 5) / bound_ref[0:1, :]
    for f in range(fields):
        data = got_ref[:, f].reshape(points, cols)
        spec = jnp.dot(up_ref[...], data, preferred_element_type=F32) + jnp.dot(
            lo_ref[...], data, preferred_element_type=F32)
        out_ref[f] = encode(spec, inverse_floor, SPECTRUM_OCTAVES)


def transform(up, lo, got, bound):
    rows, points = up.shape
    fields, cols = got.shape[1], got.shape[3]
    block = rows // 4
    return pl.pallas_call(
        transform_kernel,
        grid=(rows // block,),
        in_specs=[pl.BlockSpec((block, points), lambda i: (i, 0)),
                  pl.BlockSpec((block, points), lambda i: (i, 0)),
                  pl.BlockSpec(got.shape, lambda i: (0, 0, 0, 0)),
                  pl.BlockSpec(bound.shape, lambda i: (0, 0))],
        out_specs=pl.BlockSpec((fields, block, cols), lambda i: (0, i, 0)),
        out_shape=jax.ShapeDtypeStruct((fields, rows, cols), BF16),
        compiler_params=pltpu.CompilerParams(vmem_limit_bytes=48 << 20),
    )(up, lo, got, bound)


def solve_kernel(rblock, nrad, codes_ref, bound_ref, diff_ref, af_ref, ai_ref, qeig_ref, rf_ref, rb_ref, reig_ref,
                 out_ref, dec, x):
    f = pl.program_id(0)
    nr, nz = x.shape[1], x.shape[2]
    cols = codes_ref.shape[2]
    halves = nz // cols
    stride = halves * nrad * 2
    floor = bound_ref[0:1, :] * 2.0 ** (5 - SPECTRUM_OCTAVES)
    dec[...] = decode(codes_ref[0], floor, SPECTRUM_OCTAVES)
    for c in range(2):
        for s in range(nrad):
            for h in range(halves):
                x[c, s * rblock:(s + 1) * rblock, h * cols:(h + 1) * cols] = dec[
                    pl.ds(h * nrad * 2 + s * 2 + c, rblock, stride=stride), :]
    af, ai = split(af_ref[...]), split(ai_ref[...])
    rf, rb = split(rf_ref[0]), split(rb_ref[0])
    axial = dot3(split(x[...].reshape(2 * nr, nz)), af, NT_)
    inverse = 1.0 + diff_ref[f] * (reig_ref[...] + qeig_ref[...])
    returned = []
    for c in range(2):
        scaled = dot3(rf, split(axial[c * nr:(c + 1) * nr]), NN) / inverse
        returned.append(dot3(rb, split(scaled), NN))
    out = [dot3(split(r), ai, NT_) for r in returned]
    top = jnp.maximum(jnp.max(jnp.abs(out[0]), axis=0, keepdims=True), jnp.max(jnp.abs(out[1]), axis=0, keepdims=True))
    top = jnp.broadcast_to(jnp.max(top, axis=1, keepdims=True), (16, nz))
    top = (jnp.maximum(top, 1e-30) * 1.01).astype(BF16)
    inverse_floor = 2.0 ** SOLVED_OCTAVES / top[0:1].astype(F32)
    for c in range(2):
        code = encode(out[c], inverse_floor, SOLVED_OCTAVES)
        for s in range(nrad):
            out_ref[s, 0, c * rblock:(c + 1) * rblock, :] = code[s * rblock:(s + 1) * rblock]
    for s in range(nrad):
        out_ref[s, 0, 2 * rblock:, :] = top


def solve(codes, bound, diffusion, af, ai, qeig, rf, rb, reig, rblock, nrad):
    fields, rows, cols = codes.shape
    nr, nz = rblock * nrad, af.shape[0]

    def whole(a):
        return pl.BlockSpec(a.shape, lambda f: (0,) * a.ndim)

    return pl.pallas_call(
        functools.partial(solve_kernel, rblock, nrad),
        grid=(fields,),
        in_specs=[pl.BlockSpec((1, rows, cols), lambda f: (f, 0, 0)), whole(bound),
                  pl.BlockSpec(memory_space=pltpu.SMEM), whole(af), whole(ai), whole(qeig), whole(rf), whole(rb),
                  whole(reig)],
        out_specs=pl.BlockSpec((nrad, 1, 2 * rblock + 16, nz), lambda f: (0, f, 0, 0)),
        out_shape=jax.ShapeDtypeStruct((nrad, fields, 2 * rblock + 16, nz), BF16),
        scratch_shapes=[pltpu.VMEM((rows, cols), F32), pltpu.VMEM((2, nr, nz), F32)],
        compiler_params=pltpu.CompilerParams(vmem_limit_bytes=48 << 20),
    )(codes, bound, diffusion, af, ai, qeig, rf, rb, reig)


def unpack_kernel(rblock, codes_ref, out_ref):
    for f in range(codes_ref.shape[1]):
        floor = codes_ref[0, f, 2 * rblock:2 * rblock + 1, :].astype(F32) * 2.0 ** -SOLVED_OCTAVES
        for c in range(2):
            out_ref[f, 0, c] = decode(codes_ref[0, f, c * rblock:(c + 1) * rblock, :], floor, SOLVED_OCTAVES)


def unpack(codes, rblock):
    nrad, fields, rows, nz = codes.shape
    return pl.pallas_call(
        functools.partial(unpack_kernel, rblock),
        grid=(nrad,),
        in_specs=[pl.BlockSpec((1, fields, rows, nz), lambda s: (s, 0, 0, 0))],
        out_specs=pl.BlockSpec((fields, 1, 2, rblock, nz), lambda s: (0, s, 0, 0, 0)),
        out_shape=jax.ShapeDtypeStruct((fields, nrad, 2, rblock, nz), F32),
    )(codes)


def per_device(forcing, diffusion, axial_forward, axial_inverse_map, axial_eigenvalues,
               radial_forward, radial_backward, radial_eigenvalues):
    fields, slab, rblock, nz = forcing.shape
    nm, nrad = lax.axis_size("modes"), lax.axis_size("rad")
    points, modes = slab * nm, nm * nrad
    cols = rblock * nz // nm
    halves = nz // cols
    bound = lax.pmax(jnp.max(jnp.abs(forcing)).astype(F32), ("modes", "rad"))
    bound = jnp.broadcast_to(jnp.maximum(bound, 1e-30), (8, cols))
    up, lo = azimuthal_tables(points, 2 * modes)
    x = forcing.reshape(fields, slab, rblock, halves, cols)
    x = x.transpose(2, 3, 0, 1, 4).reshape(nm, fields, slab, cols)
    got = lax.all_to_all(x, "modes", split_axis=0, concat_axis=0, tiled=True)
    codes = transform(up, lo, got, bound)
    codes = codes.reshape(fields, modes, 2, cols).transpose(1, 0, 2, 3)
    here = lax.all_to_all(codes, ("modes", "rad"), split_axis=0, concat_axis=0, tiled=True)
    here = here.transpose(1, 0, 2, 3).reshape(fields, 2 * modes, cols)
    back = solve(here, bound, diffusion, axial_forward, axial_inverse_map, axial_eigenvalues.reshape(1, nz),
                 radial_forward, radial_backward, radial_eigenvalues.reshape(-1, 1), rblock, nrad)
    back = lax.all_to_all(back, "rad", split_axis=0, concat_axis=0, tiled=True)
    return unpack(back, rblock)


def solution(mesh):
    in_specs = (P(None, "modes", "rad", None), P(), P(), P(), P(),
                P(("modes", "rad"), None, None), P(("modes", "rad"), None, None),
                P(("modes", "rad"), None))
    return jax.shard_map(per_device, mesh=mesh, in_specs=in_specs,
                         out_specs=P(None, "modes", None, "rad", None), check_vma=False)
```

```python
import functools
import math

import jax
import jax.numpy as jnp
from jax import lax
from jax.experimental import pallas as pl
from jax.experimental.pallas import tpu as pltpu
from jax.sharding import PartitionSpec as P

F32, BF16 = jnp.float32, jnp.bfloat16
MESH = pl.DeviceIdType.MESH
Z_LO, XS, CORES, Z_HI, YS = 8, 4, 2, 2, 4
SPECTRUM_OCTAVES, SOLVED_OCTAVES = 16, 10
TINY = 1e-30


def encode(x, inverse_floor, octaves):
    grown = jnp.log2(1.0 + jnp.abs(x) * inverse_floor)
    code = jnp.exp2(grown * (239.0 / octaves) - 120.0)
    return jnp.where(x < 0, -code, code).astype(BF16)


def decode(code, floor, octaves):
    code = code.astype(F32)
    grown = (jnp.log2(jnp.abs(code)) + 120.0) * (octaves / 239.0)
    size = (jnp.exp2(grown) - 1.0) * floor
    return jnp.where(code < 0, -size, size)


def split(x):
    high = x.astype(BF16)
    return high, (x - high.astype(F32)).astype(BF16)


def dot3(a, b, dims):
    d = functools.partial(lax.dot_general, dimension_numbers=(dims, ((), ())), preferred_element_type=F32)
    return d(a[0], b[0]) + (d(a[0], b[1]) + d(a[1], b[0]))


NN, NT_ = ((1,), (0,)), ((1,), (1,))


def mode_of(z, p):
    m = (z % Z_LO) * (XS * CORES) + p % (XS * CORES)
    return m * (Z_HI * YS) + (z // Z_LO) * YS + p // (XS * CORES)


def small_tables(points):
    t = jnp.arange(points, dtype=jnp.int32)
    turn = 2.0 * math.pi / points
    z = jnp.arange(Z_HI * Z_LO, dtype=jnp.int32)
    p = jnp.arange(YS * XS * CORES, dtype=jnp.int32)

    def angles(k):
        return ((k[:, None] * t[None, :]) % points).astype(F32) * turn

    coarse, fine = angles(mode_of(z, 0)), angles(mode_of(0, p))
    scale = 1.0 / math.sqrt(points)
    c, s = jnp.cos(fine) * scale, jnp.sin(fine) * scale
    rows = 2 * p.shape[0]
    first = jnp.stack([c, -s], axis=1).reshape(rows, points)
    second = jnp.stack([s, c], axis=1).reshape(rows, points)
    return jnp.cos(coarse), jnp.sin(coarse), first, second


def kernel(xs, cc, cs, f1, f2, diff, af, ai, qeig, rf, rb, reig, out,
           up, lo, r1, enc, r2, flat, s3, r3, x, s4, r4, mx1, mx1r, mx2, mx2r, sc, scr,
           t1_s, t1_r, mx_s, mx_r, z_s, z_r, xy_s, xy_r, t4_s, t4_r, sc_s, sc_r):
    me, rad = lax.axis_index("modes"), lax.axis_index("rad")
    fields, nm, slab, cols = xs.shape
    nrad, nz_, np_ = Z_HI * YS, Z_HI * Z_LO, YS * XS * CORES
    points = nm * slab
    rblock = XS * Z_LO
    nr, nz = rblock * nrad, CORES * cols
    inner = XS * CORES
    z, p = (rad // YS) * Z_LO + me // inner, (rad % YS) * inner + me % inner

    def at(zz, pp):
        return ((zz % Z_LO) * inner + pp % inner, (zz // Z_LO) * YS + pp // inner)

    def send(src, dst, s, r, to):
        pltpu.make_async_remote_copy(src_ref=src, dst_ref=dst, send_sem=s, recv_sem=r, device_id=to,
                                     device_id_type=MESH).start()

    def drain(ref, sem):
        pltpu.make_async_copy(ref, ref, sem).wait()

    barrier = pltpu.get_barrier_semaphore()

    @pl.loop(1, nm)
    def _(i):
        pl.semaphore_signal(barrier, inc=1, device_id=((me + i) % nm, rad), device_id_type=MESH)

    @pl.loop(1, nrad)
    def _(i):
        pl.semaphore_signal(barrier, inc=1, device_id=(me, (rad + i) % nrad), device_id_type=MESH)

    top = jnp.zeros((slab, cols), F32)
    for f in range(fields):
        top = jnp.maximum(top, jnp.max(jnp.abs(xs[f]).astype(F32), axis=0))
    top = jnp.max(jnp.max(top, axis=0, keepdims=True), axis=1, keepdims=True)
    mx1[...] = jnp.broadcast_to(top, (1, cols))
    pl.semaphore_wait(barrier, nm + nrad - 2)

    @pl.loop(1, nm)
    def _(i):
        m = (me + i) % nm
        send(mx1, mx1r.at[me], mx_s.at[0], mx_r.at[0], (m, rad))

    for f in range(fields):
        @pl.loop(1, nm)
        def _(i):
            m = (me + i) % nm
            send(xs.at[f, m], r1.at[f, me], t1_s.at[f], t1_r.at[f], (m, rad))

    mx1r[me] = mx1[...]
    for f in range(fields):
        r1[f, me] = xs[f, me]

    drain(mx1r.at[pl.ds(0, nm - 1)], mx_r.at[0])
    top = jnp.max(mx1r[...], axis=0)
    mx2[...] = top
    mx2r[rad] = top

    @pl.loop(1, nrad)
    def _(i):
        send(mx2, mx2r.at[rad], mx_s.at[1], mx_r.at[1], (me, (rad + i) % nrad))

    half = 2 * np_

    @pl.loop(0, nz_)
    def _(a):
        table = cc[pl.ds(a, 1), :] * f1[...] - cs[pl.ds(a, 1), :] * f2[...]
        high, low = split(table)
        rows = pl.ds(pl.multiple_of(a * half, half), half)
        up[rows, :] = high
        lo[rows, :] = low

    drain(mx2r.at[pl.ds(0, nrad - 1)], mx_r.at[1])
    bound = jnp.maximum(jnp.max(mx2r[...], axis=0), TINY)
    floor = bound * 2.0 ** (5 - SPECTRUM_OCTAVES)
    inverse_floor = 2.0 ** (SPECTRUM_OCTAVES - 5) / bound
    blocks = 4
    each = nz_ // blocks

    def transform(f):
        drain(r1.at[f, pl.ds(0, nm - 1)], t1_r.at[f])
        data = r1[f].reshape(points, cols)

        @pl.loop(0, blocks)
        def _(b):
            rows = pl.ds(pl.multiple_of(b * each * half, each * half), each * half)
            spec = jnp.dot(up[rows, :], data, preferred_element_type=F32) + jnp.dot(
                lo[rows, :], data, preferred_element_type=F32)
            enc[f, pl.ds(b * each, each)] = encode(spec, inverse_floor, SPECTRUM_OCTAVES).reshape(each, half, cols)

        @pl.loop(1, nz_)
        def _(i):
            to = (z + i) % nz_
            send(enc.at[f, to], r2.at[f, z], z_s.at[f], z_r.at[f], at(to, p))

        r2[f, z] = enc[f, z]

    def regroup(f):
        drain(r2.at[f, pl.ds(0, nz_ - 1)], z_r.at[f])
        flat[...] = r2[f].astype(F32).reshape(nz_ * half, cols)
        for q in range(np_):
            for c in range(2):
                s3[f, q, c * nz_:(c + 1) * nz_, :] = flat[pl.ds(2 * q + c, nz_, stride=half), :].astype(BF16)

        @pl.loop(1, np_)
        def _(i):
            to = (p + i) % np_
            send(s3.at[f, to], r3.at[f, p], xy_s.at[f], xy_r.at[f], at(z, to))

        r3[f, p] = s3[f, p]

    def solve(f):
        drain(r3.at[f, pl.ds(0, np_ - 1)], xy_r.at[f])
        for q in range(np_):
            y, xx, core = q // inner, (q // CORES) % XS, q % CORES
            value = decode(r3[f, q], floor, SPECTRUM_OCTAVES)
            for c in range(2):
                for h in range(Z_HI):
                    r0 = (h * YS + y) * rblock + xx * Z_LO
                    x[c, r0:r0 + Z_LO, core * cols:(core + 1) * cols] = value[
                        c * nz_ + h * Z_LO:c * nz_ + (h + 1) * Z_LO]
        axial = dot3(split(x[...].reshape(2 * nr, nz)), split(af[...]), NT_)
        denominator = 1.0 + diff[f] * (reig[...] + qeig[...])
        result = []
        for c in range(2):
            scaled = dot3(split(rf[0]), split(axial[c * nr:(c + 1) * nr]), NN) / denominator
            result.append(dot3(split(dot3(split(rb[0]), split(scaled), NN)), split(ai[...]), NT_))
        top = jnp.maximum(jnp.max(jnp.abs(result[0]), axis=0, keepdims=True),
                          jnp.max(jnp.abs(result[1]), axis=0, keepdims=True))
        top = jnp.maximum(jnp.broadcast_to(jnp.max(top, axis=1, keepdims=True), (1, nz)), TINY)
        sc[f] = top
        scr[f, rad] = top
        inverse = 2.0 ** SOLVED_OCTAVES / top
        for c in range(2):
            code = encode(result[c], inverse, SOLVED_OCTAVES)
            for s in range(nrad):
                s4[f, s, c] = code[s * rblock:(s + 1) * rblock]

        @pl.loop(1, nrad)
        def _(i):
            to = (rad + i) % nrad
            send(sc.at[f], scr.at[f, rad], sc_s.at[f], sc_r.at[f], (me, to))
            send(s4.at[f, to], r4.at[f, rad], t4_s.at[f], t4_r.at[f], (me, to))

        r4[f, rad] = s4[f, rad]

    def unpack(f):
        drain(scr.at[f, pl.ds(0, nrad - 1)], sc_r.at[f])
        drain(r4.at[f, pl.ds(0, nrad - 1)], t4_r.at[f])

        @pl.loop(0, nrad)
        def _(s):
            low = scr[f, s] * 2.0 ** -SOLVED_OCTAVES
            for c in range(2):
                out[f, s, c] = decode(r4[f, s, c], low, SOLVED_OCTAVES)

    transform(0)
    transform(1)
    regroup(0)
    transform(2)
    regroup(1)
    solve(0)
    regroup(2)
    solve(1)
    solve(2)
    for f in range(fields):
        unpack(f)

    drain(mx1r.at[pl.ds(0, nm - 1)], mx_s.at[0])
    drain(mx2r.at[pl.ds(0, nrad - 1)], mx_s.at[1])
    for f in range(fields):
        drain(r1.at[f, pl.ds(0, nm - 1)], t1_s.at[f])
        drain(r2.at[f, pl.ds(0, nz_ - 1)], z_s.at[f])
        drain(r3.at[f, pl.ds(0, np_ - 1)], xy_s.at[f])
        drain(scr.at[f, pl.ds(0, nrad - 1)], sc_s.at[f])
        drain(r4.at[f, pl.ds(0, nrad - 1)], t4_s.at[f])


def per_device(forcing, diffusion, axial_forward, axial_inverse_map, axial_eigenvalues,
               radial_forward, radial_backward, radial_eigenvalues):
    fields, slab, rblock, nz = forcing.shape
    nm, nrad = lax.axis_size("modes"), lax.axis_size("rad")
    points, cols = slab * nm, nz // CORES
    nzs, nps = Z_HI * Z_LO, YS * XS * CORES
    xs = forcing.reshape(fields, slab, XS, Z_LO, CORES, cols).transpose(0, 3, 2, 4, 1, 5)
    xs = xs.reshape(fields, nm, slab, cols)
    tables = small_tables(points)
    dma = pltpu.SemaphoreType.DMA
    vmem = pl.BlockSpec(memory_space=pltpu.VMEM)
    args = (xs, *tables, diffusion, axial_forward, axial_inverse_map, axial_eigenvalues.reshape(1, nz),
            radial_forward, radial_backward, radial_eigenvalues.reshape(-1, 1))
    specs = [vmem] * len(args)
    specs[5] = pl.BlockSpec(memory_space=pltpu.SMEM)
    return pl.pallas_call(
        kernel,
        out_shape=jax.ShapeDtypeStruct((fields, nrad, 2, rblock, nz), F32),
        in_specs=specs,
        out_specs=vmem,
        scratch_shapes=[
            pltpu.VMEM((2 * nzs * nps, points), BF16), pltpu.VMEM((2 * nzs * nps, points), BF16),
            pltpu.VMEM((fields, nm, slab, cols), BF16),
            pltpu.VMEM((fields, nzs, 2 * nps, cols), BF16), pltpu.VMEM((fields, nzs, 2 * nps, cols), BF16),
            pltpu.VMEM((nzs * 2 * nps, cols), F32),
            pltpu.VMEM((fields, nps, 2 * nzs, cols), BF16), pltpu.VMEM((fields, nps, 2 * nzs, cols), BF16),
            pltpu.VMEM((2, rblock * nrad, nz), F32),
            pltpu.VMEM((fields, nrad, 2, rblock, nz), BF16), pltpu.VMEM((fields, nrad, 2, rblock, nz), BF16),
            pltpu.VMEM((1, cols), F32), pltpu.VMEM((nm, 1, cols), F32),
            pltpu.VMEM((1, cols), F32), pltpu.VMEM((nrad, 1, cols), F32),
            pltpu.VMEM((fields, 1, nz), F32), pltpu.VMEM((fields, nrad, 1, nz), F32),
            dma((fields,)), dma((fields,)), dma((2,)), dma((2,)), dma((fields,)), dma((fields,)),
            dma((fields,)), dma((fields,)), dma((fields,)), dma((fields,)), dma((fields,)), dma((fields,)),
        ],
        compiler_params=pltpu.CompilerParams(collective_id=0, has_side_effects=True, vmem_limit_bytes=56 << 20),
    )(*args)


def solution(mesh):
    in_specs = (P(None, "modes", "rad", None), P(), P(), P(), P(),
                P(("modes", "rad"), None, None), P(("modes", "rad"), None, None),
                P(("modes", "rad"), None))
    return jax.shard_map(per_device, mesh=mesh, in_specs=in_specs,
                         out_specs=P(None, "modes", None, "rad", None), check_vma=False)
```

```python
import functools
import math

import jax
import jax.numpy as jnp
import numpy as np
from jax import lax
from jax.experimental import pallas as pl
from jax.experimental.pallas import tpu as pltpu
from jax.sharding import PartitionSpec as P

F32, BF16 = jnp.float32, jnp.bfloat16
MESH = pl.DeviceIdType.MESH
Z_LO, XS, CORES, Z_HI, YS = 8, 4, 2, 2, 4
SPECTRUM_OCTAVES, SOLVED_OCTAVES = 16, 10
TINY = 1e-30


def encode(x, inverse_floor, octaves):
    grown = jnp.log2(1.0 + jnp.abs(x) * inverse_floor)
    code = jnp.exp2(grown * (239.0 / octaves) - 120.0)
    return jnp.where(x < 0, -code, code).astype(BF16)


def decode(code, floor, octaves):
    code = code.astype(F32)
    grown = (jnp.log2(jnp.abs(code)) + 120.0) * (octaves / 239.0)
    size = (jnp.exp2(grown) - 1.0) * floor
    return jnp.where(code < 0, -size, size)


def split(x):
    high = x.astype(BF16)
    return high, (x - high.astype(F32)).astype(BF16)


def dot3(a, b, dims):
    d = functools.partial(lax.dot_general, dimension_numbers=(dims, ((), ())), preferred_element_type=F32)
    return d(a[0], b[0]) + (d(a[0], b[1]) + d(a[1], b[0]))


NN, NT_ = ((1,), (0,)), ((1,), (1,))


def mode_of(z, p):
    m = (z % Z_LO) * (XS * CORES) + p % (XS * CORES)
    return m * (Z_HI * YS) + (z // Z_LO) * YS + p // (XS * CORES)


def small_tables(points):
    k = [mode_of(z, 0) for z in range(Z_HI * Z_LO)] + [mode_of(0, p) for p in range(YS * XS * CORES)]
    turns = np.outer(np.array(k), np.arange(points)) % points
    radians = turns * (2.0 * math.pi / points)
    return np.cos(radians).astype(np.float32), np.sin(radians).astype(np.float32)


def kernel(forcing, cosine, sine, diff, af, ai, qeig, rf, rb, reig, out,
           up, lo, r1, enc, r2, flat, s3, r3, x, s4, r4, mx1, mx1r, mx2, mx2r, sc, scr,
           t1_s, t1_r, mx_s, mx_r, z_s, z_r, xy_s, xy_r, t4_s, t4_r, sc_s, sc_r, rp, rp_s, rp_r, fw_s, eigen, xs, wide, ob, out_s):
    me, rad = lax.axis_index("modes"), lax.axis_index("rad")
    fields, nm, slab, cols = xs.shape
    nrad, nz_, np_ = Z_HI * YS, Z_HI * Z_LO, YS * XS * CORES
    points = nm * slab
    rblock = XS * Z_LO
    nr, nz = rblock * nrad, CORES * cols
    inner = XS * CORES
    z, p = (rad // YS) * Z_LO + me // inner, (rad % YS) * inner + me % inner

    def at(zz, pp):
        return ((zz % Z_LO) * inner + pp % inner, (zz // Z_LO) * YS + pp // inner)

    def send(src, dst, s, r, to):
        pltpu.make_async_remote_copy(src_ref=src, dst_ref=dst, send_sem=s, recv_sem=r, device_id=to,
                                     device_id_type=MESH).start()

    def drain(ref, sem):
        pltpu.make_async_copy(ref, ref, sem).wait()

    barrier = pltpu.get_barrier_semaphore()

    @pl.loop(1, nm)
    def _(i):
        pl.semaphore_signal(barrier, inc=1, device_id=((me + i) % nm, rad), device_id_type=MESH)

    @pl.loop(1, nrad)
    def _(i):
        pl.semaphore_signal(barrier, inc=1, device_id=(me, (rad + i) % nrad), device_id_type=MESH)

    def spread(f):
        for core in range(CORES):
            wide[core] = forcing[f, :, :, core * cols:(core + 1) * cols].astype(F32).reshape(slab * rblock, cols)
        for m in range(nm):
            row = m // CORES % XS * Z_LO + m // inner
            xs[f, m] = wide[m % CORES, pl.ds(row, slab, stride=rblock), :].astype(BF16)

    def begin(f):
        @pl.loop(1, nm)
        def _(i):
            m = (me + i) % nm
            send(xs.at[f, m], r1.at[f, me], t1_s.at[f], t1_r.at[f], (m, rad))

    spread(0)
    pl.semaphore_wait(barrier, nm + nrad - 2)
    begin(0)
    top = jnp.zeros((slab, cols), F32)
    for f in range(fields):
        for core in range(CORES):
            top = jnp.maximum(top, jnp.max(
                jnp.abs(forcing[f, :, :, core * cols:(core + 1) * cols].astype(F32)), axis=1))
    top = jnp.max(jnp.max(top, axis=0, keepdims=True), axis=1, keepdims=True)
    mx1[...] = jnp.broadcast_to(top, (1, cols))

    @pl.loop(1, nm)
    def _(i):
        m = (me + i) % nm
        send(mx1, mx1r.at[me], mx_s.at[0], mx_r.at[0], (m, rad))

    for f in range(1, fields):
        spread(f)
        begin(f)
    mx1r[me] = mx1[...]
    for f in range(fields):
        r1[f, me] = xs[f, me]

    drain(mx1r.at[pl.ds(0, nm - 1)], mx_r.at[0])
    top = jnp.max(mx1r[...], axis=0)
    mx2[...] = top
    mx2r[rad] = top

    @pl.loop(1, nrad)
    def _(i):
        send(mx2, mx2r.at[rad], mx_s.at[1], mx_r.at[1], (me, (rad + i) % nrad))

    half, hop, scale = 2 * np_, nz_ // 4, 1.0 / math.sqrt(points)
    eigen[...] = jnp.transpose(jnp.broadcast_to(reig[...], (nz, nr))) + qeig[...]

    @pl.loop(0, nz_)
    def _(a):
        ca, sa = cosine[pl.ds(a, 1), :] * scale, sine[pl.ds(a, 1), :] * scale
        cb, sb = cosine[nz_:, :], sine[nz_:, :]
        for c, table in enumerate((ca * cb - sa * sb, -(sa * cb + ca * sb))):
            high, low = split(table)
            rows = pl.ds(pl.multiple_of(a * half + c * np_, np_), np_)
            up[rows, :] = high
            lo[rows, :] = low

    drain(mx2r.at[pl.ds(0, nrad - 1)], mx_r.at[1])
    bound = jnp.maximum(jnp.max(mx2r[...], axis=0), TINY)
    floor = bound * 2.0 ** (5 - SPECTRUM_OCTAVES)
    inverse_floor = 2.0 ** (SPECTRUM_OCTAVES - 5) / bound
    blocks = 4
    each = nz_ // blocks

    def transform(f):
        drain(r1.at[f, pl.ds(0, nm - 1)], t1_r.at[f])
        data = r1[f].reshape(points, cols)

        @pl.loop(0, blocks)
        def _(b):
            rows = pl.ds(pl.multiple_of(b * each * half, each * half), each * half)
            spec = jnp.dot(up[rows, :], data, preferred_element_type=F32) + jnp.dot(
                lo[rows, :], data, preferred_element_type=F32)
            enc[f, pl.ds(b * each, each)] = encode(spec, inverse_floor, SPECTRUM_OCTAVES).reshape(each, half, cols)

        @pl.loop(1, nz_)
        def _(i):
            to = (z + i) % nz_
            send(enc.at[f, to], r2.at[f, z], z_s.at[f], z_r.at[f], at(to, p))

        r2[f, z] = enc[f, z]

    def regroup(f):
        drain(r2.at[f, pl.ds(0, nz_ - 1)], z_r.at[f])
        flat[...] = r2[f].astype(F32).reshape(nz_ * half, cols)
        for q in range(np_):
            for c in range(2):
                s3[f, q, c * nz_:(c + 1) * nz_, :] = flat[pl.ds(c * np_ + q, nz_, stride=half), :].astype(BF16)

        @pl.loop(1, np_)
        def _(i):
            to = (p + i) % np_
            send(s3.at[f, to], r3.at[f, p], xy_s.at[f], xy_r.at[f], at(z, to))

        r3[f, p] = s3[f, p]

    def solve(f):
        drain(r3.at[f, pl.ds(0, np_ - 1)], xy_r.at[f])
        for q in range(np_):
            y, xx, core = q // inner, (q // CORES) % XS, q % CORES
            value = decode(r3[f, q], floor, SPECTRUM_OCTAVES)
            for c in range(2):
                for h in range(Z_HI):
                    r0 = (h * YS + y) * rblock + xx * Z_LO
                    x[c, r0:r0 + Z_LO, core * cols:(core + 1) * cols] = value[
                        c * nz_ + h * Z_LO:c * nz_ + (h + 1) * Z_LO]
        axial = dot3(split(x[...].reshape(2 * nr, nz)), split(af[...]), NT_)
        denominator = 1.0 + diff[f] * eigen[...]
        result = []
        for c in range(2):
            scaled = dot3(split(rf[0]), split(axial[c * nr:(c + 1) * nr]), NN) / denominator
            result.append(dot3(split(dot3(split(rb[0]), split(scaled), NN)), split(ai[...]), NT_))
        top = jnp.maximum(jnp.max(jnp.abs(result[0]), axis=0, keepdims=True),
                          jnp.max(jnp.abs(result[1]), axis=0, keepdims=True))
        top = jnp.maximum(jnp.broadcast_to(jnp.max(top, axis=1, keepdims=True), (1, nz)), TINY)
        sc[f] = top
        scr[f, rad] = top
        inverse = 2.0 ** SOLVED_OCTAVES / top
        for c in range(2):
            code = encode(result[c], inverse, SOLVED_OCTAVES)
            for s in range(nrad):
                s4[f, s, c] = code[s * rblock:(s + 1) * rblock]

        far = (1 - rad // YS) * YS

        @pl.loop(0, YS)
        def _(y):
            send(s4.at[f, far + y, 0], rp.at[f, 0, rad % YS], rp_s.at[f], rp_r.at[f, 0],
                 at((z + hop) % nz_, y * inner + p % inner))
            send(s4.at[f, far + y, 1], rp.at[f, 1, rad % YS], rp_s.at[f], rp_r.at[f, 1],
                 at((z + nz_ - hop) % nz_, y * inner + p % inner))

        @pl.loop(1, YS)
        def _(i):
            to = rad // YS * YS + (rad + i) % YS
            send(s4.at[f, to], r4.at[f, rad], t4_s.at[f], t4_r.at[f], (me, to))

        @pl.loop(1, nrad)
        def _(i):
            send(sc.at[f], scr.at[f, rad], sc_s.at[f], sc_r.at[f], (me, (rad + i) % nrad))

        r4[f, rad] = s4[f, rad]

    def relay(f):
        for part, step in ((0, hop), (1, nz_ - hop)):
            drain(rp.at[f, part], rp_r.at[f, part])
            source = (z + nz_ - step) % nz_ // Z_LO * YS
            send(rp.at[f, part], r4.at[f, pl.ds(source, YS), part], fw_s.at[f], t4_r.at[f], at((z + step) % nz_, p))

    def unpack(f):
        drain(scr.at[f, pl.ds(0, nrad - 1)], sc_r.at[f])
        drain(r4.at[f, pl.ds(0, nrad - 1)], t4_r.at[f])

        @pl.loop(0, nrad)
        def _(s):
            low = scr[f, s] * 2.0 ** -SOLVED_OCTAVES
            for c in range(2):
                ob[f, s, c] = decode(r4[f, s, c], low, SOLVED_OCTAVES)

        pltpu.make_async_copy(ob.at[f], out.at[f], out_s.at[f]).start()

    transform(0)
    transform(1)
    regroup(0)
    transform(2)
    regroup(1)
    solve(0)
    regroup(2)
    solve(1)
    relay(0)
    solve(2)
    relay(1)
    unpack(0)
    relay(2)
    unpack(1)
    unpack(2)
    for f in range(fields):
        pltpu.make_async_copy(ob.at[f], out.at[f], out_s.at[f]).wait()

    drain(mx1r.at[pl.ds(0, nm - 1)], mx_s.at[0])
    drain(mx2r.at[pl.ds(0, nrad - 1)], mx_s.at[1])
    for f in range(fields):
        drain(r1.at[f, pl.ds(0, nm - 1)], t1_s.at[f])
        drain(r2.at[f, pl.ds(0, nz_ - 1)], z_s.at[f])
        drain(r3.at[f, pl.ds(0, np_ - 1)], xy_s.at[f])
        drain(scr.at[f, pl.ds(0, nrad - 1)], sc_s.at[f])
        drain(r4.at[f, pl.ds(0, YS - 1)], t4_s.at[f])
        drain(r4.at[f, pl.ds(0, YS)], rp_s.at[f])
        drain(r4.at[f, pl.ds(0, YS)], fw_s.at[f])


def per_device(forcing, diffusion, axial_forward, axial_inverse_map, axial_eigenvalues,
               radial_forward, radial_backward, radial_eigenvalues):
    fields, slab, rblock, nz = forcing.shape
    nm, nrad = lax.axis_size("modes"), lax.axis_size("rad")
    points, cols = slab * nm, nz // CORES
    nzs, nps = Z_HI * Z_LO, YS * XS * CORES
    tables = [jnp.asarray(t) for t in small_tables(points)]
    dma = pltpu.SemaphoreType.DMA
    vmem = pl.BlockSpec(memory_space=pltpu.VMEM)
    args = (forcing, *tables, diffusion, axial_forward, axial_inverse_map, axial_eigenvalues.reshape(1, nz),
            radial_forward, radial_backward, radial_eigenvalues)
    specs = [vmem] * len(args)
    specs[3] = pl.BlockSpec(memory_space=pltpu.SMEM)
    return pl.pallas_call(
        kernel,
        out_shape=jax.ShapeDtypeStruct((fields, nrad, 2, rblock, nz), F32),
        in_specs=specs,
        out_specs=pl.BlockSpec(memory_space=pl.ANY),
        scratch_shapes=[
            pltpu.VMEM((2 * nzs * nps, points), BF16), pltpu.VMEM((2 * nzs * nps, points), BF16),
            pltpu.VMEM((fields, nm, slab, cols), BF16),
            pltpu.VMEM((fields, nzs, 2 * nps, cols), BF16), pltpu.VMEM((fields, nzs, 2 * nps, cols), BF16),
            pltpu.VMEM((nzs * 2 * nps, cols), F32),
            pltpu.VMEM((fields, nps, 2 * nzs, cols), BF16), pltpu.VMEM((fields, nps, 2 * nzs, cols), BF16),
            pltpu.VMEM((2, rblock * nrad, nz), F32),
            pltpu.VMEM((fields, nrad, 2, rblock, nz), BF16), pltpu.VMEM((fields, nrad, 2, rblock, nz), BF16),
            pltpu.VMEM((1, cols), F32), pltpu.VMEM((nm, 1, cols), F32),
            pltpu.VMEM((1, cols), F32), pltpu.VMEM((nrad, 1, cols), F32),
            pltpu.VMEM((fields, 1, nz), F32), pltpu.VMEM((fields, nrad, 1, nz), F32),
            dma((fields,)), dma((fields,)), dma((2,)), dma((2,)), dma((fields,)), dma((fields,)),
            dma((fields,)), dma((fields,)), dma((fields,)), dma((fields,)), dma((fields,)), dma((fields,)),
            pltpu.VMEM((fields, 2, YS, rblock, nz), BF16), dma((fields,)), dma((fields, 2)), dma((fields,)),
            pltpu.VMEM((rblock * nrad, nz), F32), pltpu.VMEM((fields, nm, slab, cols), BF16),
            pltpu.VMEM((CORES, slab * rblock, cols), F32), pltpu.VMEM((fields, nrad, 2, rblock, nz), F32), dma((fields,)),
        ],
        compiler_params=pltpu.CompilerParams(collective_id=0, has_side_effects=True, vmem_limit_bytes=56 << 20),
    )(*args)


def solution(mesh):
    in_specs = (P(None, "modes", "rad", None), P(), P(), P(), P(),
                P(("modes", "rad"), None, None), P(("modes", "rad"), None, None),
                P(("modes", "rad"), None))
    return jax.shard_map(per_device, mesh=mesh, in_specs=in_specs,
                         out_specs=P(None, "modes", None, "rad", None), check_vma=False)
```

```python
import functools
import math

import jax
import jax.numpy as jnp
import numpy as np
from jax import lax
from jax.experimental import pallas as pl
from jax.experimental.pallas import tpu as pltpu
from jax.sharding import PartitionSpec as P

F32, BF16 = jnp.float32, jnp.bfloat16
MESH = pl.DeviceIdType.MESH
Z_LO, XS, CORES, Z_HI, YS = 8, 4, 2, 2, 4
SPECTRUM_OCTAVES, SOLVED_OCTAVES = 16, 10
TINY = 1e-30


def encode(x, inverse_floor, octaves):
    grown = jnp.log2(1.0 + jnp.abs(x) * inverse_floor)
    code = jnp.exp2(grown * (239.0 / octaves) - 120.0)
    return jnp.where(x < 0, -code, code).astype(BF16)


def decode(code, floor, octaves):
    code = code.astype(F32)
    grown = (jnp.log2(jnp.abs(code)) + 120.0) * (octaves / 239.0)
    size = (jnp.exp2(grown) - 1.0) * floor
    return jnp.where(code < 0, -size, size)


def split(x):
    high = x.astype(BF16)
    return high, (x - high.astype(F32)).astype(BF16)


def dot3(a, b, dims):
    d = functools.partial(lax.dot_general, dimension_numbers=(dims, ((), ())), preferred_element_type=F32)
    return d(a[0], b[0]) + (d(a[0], b[1]) + d(a[1], b[0]))


NN, NT_ = ((1,), (0,)), ((1,), (1,))


def mode_of(z, p):
    m = (z % Z_LO) * (XS * CORES) + p % (XS * CORES)
    return m * (Z_HI * YS) + (z // Z_LO) * YS + p // (XS * CORES)


def small_tables(points):
    k = [mode_of(z, 0) for z in range(Z_HI * Z_LO)] + [mode_of(0, p) for p in range(YS * XS * CORES)]
    turns = np.outer(np.array(k), np.arange(points)) % points
    radians = turns * (2.0 * math.pi / points)
    return np.cos(radians).astype(np.float32), np.sin(radians).astype(np.float32)


def kernel(forcing_, cosine_, sine_, diff_, af_, ai_, qeig_, rf_, rb_, reig_, out,
           up, lo, r1, enc, r2, flat, s3, r3, x, s4, r4, mx1, mx1r, mx2, mx2r, sc, scr,
           t1_s, t1_r, mx_s, mx_r, z_s, z_r, xy_s, xy_r, t4_s, t4_r, sc_s, sc_r, rp, rp_s, rp_r, fw_s, eigen, xs, wide,
           forcing, cosine, sine, diff, af, ai, qeig, rf, rb, reig, in_s):
    me, rad = lax.axis_index("modes"), lax.axis_index("rad")
    fields, nm, slab, cols = xs.shape
    nrad, nz_, np_ = Z_HI * YS, Z_HI * Z_LO, YS * XS * CORES
    points = nm * slab
    rblock = XS * Z_LO
    nr, nz = rblock * nrad, CORES * cols
    inner = XS * CORES
    z, p = (rad // YS) * Z_LO + me // inner, (rad % YS) * inner + me % inner

    def at(zz, pp):
        return ((zz % Z_LO) * inner + pp % inner, (zz // Z_LO) * YS + pp // inner)

    def send(src, dst, s, r, to):
        pltpu.make_async_remote_copy(src_ref=src, dst_ref=dst, send_sem=s, recv_sem=r, device_id=to,
                                     device_id_type=MESH).start()

    def drain(ref, sem):
        pltpu.make_async_copy(ref, ref, sem).wait()

    loads = [pltpu.make_async_copy(forcing_, forcing, in_s.at[0])]
    for n, (src, dst) in enumerate(((cosine_, cosine), (sine_, sine), (diff_, diff), (af_, af), (ai_, ai), (qeig_, qeig), (rf_, rf),
                                  (rb_, rb), (reig_, reig))):
        loads.append(pltpu.make_async_copy(src, dst, in_s.at[n + 1]))
    for load in loads:
        load.start()
    barrier = pltpu.get_barrier_semaphore()

    @pl.loop(1, nm)
    def _(i):
        pl.semaphore_signal(barrier, inc=1, device_id=((me + i) % nm, rad), device_id_type=MESH)

    @pl.loop(1, nrad)
    def _(i):
        pl.semaphore_signal(barrier, inc=1, device_id=(me, (rad + i) % nrad), device_id_type=MESH)

    def spread(f):
        for core in range(CORES):
            wide[core] = forcing[f, :, :, core * cols:(core + 1) * cols].astype(F32).reshape(slab * rblock, cols)
        for m in range(nm):
            row = m // CORES % XS * Z_LO + m // inner
            xs[f, m] = wide[m % CORES, pl.ds(row, slab, stride=rblock), :].astype(BF16)

    def begin(f):
        @pl.loop(1, nm)
        def _(i):
            m = (me + i) % nm
            send(xs.at[f, m], r1.at[f, me], t1_s.at[f], t1_r.at[f], (m, rad))

    loads[0].wait()
    top = jnp.zeros((slab, cols), F32)
    for f in range(fields):
        for core in range(CORES):
            top = jnp.maximum(top, jnp.max(
                jnp.abs(forcing[f, :, :, core * cols:(core + 1) * cols].astype(F32)), axis=1))
    top = jnp.max(jnp.max(top, axis=0, keepdims=True), axis=1, keepdims=True)
    mx1[...] = jnp.broadcast_to(top, (1, cols))
    spread(0)
    pl.semaphore_wait(barrier, nm + nrad - 2)

    @pl.loop(1, nm)
    def _(i):
        send(mx1, mx1r.at[me], mx_s.at[0], mx_r.at[0], ((me + i) % nm, rad))

    begin(0)
    mx1r[me] = mx1[...]
    spread(1)
    drain(mx1r.at[pl.ds(0, nm - 1)], mx_r.at[0])
    top = jnp.max(mx1r[...], axis=0)
    mx2[...] = top
    mx2r[rad] = top

    @pl.loop(1, nrad)
    def _(i):
        send(mx2, mx2r.at[rad], mx_s.at[1], mx_r.at[1], (me, (rad + i) % nrad))

    begin(1)
    spread(2)
    begin(2)
    for f in range(fields):
        r1[f, me] = xs[f, me]

    for load in loads[1:]:
        load.wait()
    half, hop, scale = 2 * np_, nz_ // 4, 1.0 / math.sqrt(points)
    eigen[...] = jnp.transpose(jnp.broadcast_to(reig[...], (nz, nr))) + qeig[...]

    @pl.loop(0, nz_)
    def _(a):
        ca, sa = cosine[pl.ds(a, 1), :] * scale, sine[pl.ds(a, 1), :] * scale
        cb, sb = cosine[nz_:, :], sine[nz_:, :]
        for c, table in enumerate((ca * cb - sa * sb, -(sa * cb + ca * sb))):
            high, low = split(table)
            rows = pl.ds(pl.multiple_of(a * half + c * np_, np_), np_)
            up[rows, :] = high
            lo[rows, :] = low

    drain(mx2r.at[pl.ds(0, nrad - 1)], mx_r.at[1])
    bound = jnp.maximum(jnp.max(mx2r[...], axis=0), TINY)
    floor = bound * 2.0 ** (5 - SPECTRUM_OCTAVES)
    inverse_floor = 2.0 ** (SPECTRUM_OCTAVES - 5) / bound
    blocks = 4
    each = nz_ // blocks

    def transform(f):
        drain(r1.at[f, pl.ds(0, nm - 1)], t1_r.at[f])
        data = r1[f].reshape(points, cols)

        @pl.loop(0, blocks)
        def _(b):
            rows = pl.ds(pl.multiple_of(b * each * half, each * half), each * half)
            spec = jnp.dot(up[rows, :], data, preferred_element_type=F32) + jnp.dot(
                lo[rows, :], data, preferred_element_type=F32)
            enc[f, pl.ds(b * each, each)] = encode(spec, inverse_floor, SPECTRUM_OCTAVES).reshape(each, half, cols)
        r2[f, z] = enc[f, z]

    def send_z(f, i):
        to = (z + i) % nz_
        send(enc.at[f, to], r2.at[f, z], z_s.at[f], z_r.at[f], at(to, p))

    def regroup(f):
        drain(r2.at[f, pl.ds(0, nz_ - 1)], z_r.at[f])
        flat[...] = r2[f].astype(F32).reshape(nz_ * half, cols)
        for q in range(np_):
            for c in range(2):
                s3[f, q, c * nz_:(c + 1) * nz_, :] = flat[pl.ds(c * np_ + q, nz_, stride=half), :].astype(BF16)
        r3[f, p] = s3[f, p]

    def send_xy(f, i):
        to = (p + i) % np_
        send(s3.at[f, to], r3.at[f, p], xy_s.at[f], xy_r.at[f], at(z, to))

    def solve(f):
        drain(r3.at[f, pl.ds(0, np_ - 1)], xy_r.at[f])
        for q in range(np_):
            y, xx, core = q // inner, (q // CORES) % XS, q % CORES
            value = decode(r3[f, q], floor, SPECTRUM_OCTAVES)
            for c in range(2):
                for h in range(Z_HI):
                    r0 = (h * YS + y) * rblock + xx * Z_LO
                    x[c, r0:r0 + Z_LO, core * cols:(core + 1) * cols] = value[
                        c * nz_ + h * Z_LO:c * nz_ + (h + 1) * Z_LO]
        axial = dot3(split(x[...].reshape(2 * nr, nz)), split(af[...]), NT_)
        denominator = 1.0 + diff[0:1, f:f + 1] * eigen[...]
        result = []
        for c in range(2):
            scaled = dot3(split(rf[0]), split(axial[c * nr:(c + 1) * nr]), NN) / denominator
            result.append(dot3(split(dot3(split(rb[0]), split(scaled), NN)), split(ai[...]), NT_))
        top = jnp.maximum(jnp.max(jnp.abs(result[0]), axis=0, keepdims=True),
                          jnp.max(jnp.abs(result[1]), axis=0, keepdims=True))
        top = jnp.maximum(jnp.broadcast_to(jnp.max(top, axis=1, keepdims=True), (1, nz)), TINY)
        sc[f] = top
        scr[f, rad] = top
        inverse = 2.0 ** SOLVED_OCTAVES / top
        for c in range(2):
            code = encode(result[c], inverse, SOLVED_OCTAVES)
            for s in range(nrad):
                s4[f, s, c] = code[s * rblock:(s + 1) * rblock]

        r4[f, rad] = s4[f, rad]

    far = (1 - rad // YS) * YS

    def send_far(f, y):
        send(s4.at[f, far + y, 0], rp.at[f, 0, rad % YS], rp_s.at[f], rp_r.at[f, 0],
             at((z + hop) % nz_, y * inner + p % inner))
        send(s4.at[f, far + y, 1], rp.at[f, 1, rad % YS], rp_s.at[f], rp_r.at[f, 1],
             at((z + nz_ - hop) % nz_, y * inner + p % inner))

    def send_near(f):
        @pl.loop(1, nrad)
        def _(i):
            send(sc.at[f], scr.at[f, rad], sc_s.at[f], sc_r.at[f], (me, (rad + i) % nrad))

        @pl.loop(1, YS)
        def _(i):
            to = rad // YS * YS + (rad + i) % YS
            send(s4.at[f, to], r4.at[f, rad], t4_s.at[f], t4_r.at[f], (me, to))

    def relay(f):
        for part, step in ((0, hop), (1, nz_ - hop)):
            drain(rp.at[f, part], rp_r.at[f, part])
            source = (z + nz_ - step) % nz_ // Z_LO * YS
            send(rp.at[f, part], r4.at[f, pl.ds(source, YS), part], fw_s.at[f], t4_r.at[f], at((z + step) % nz_, p))

    def unpack(f):
        drain(scr.at[f, pl.ds(0, nrad - 1)], sc_r.at[f])
        drain(r4.at[f, pl.ds(0, nrad - 1)], t4_r.at[f])

        @pl.loop(0, nrad)
        def _(s):
            low = scr[f, s] * 2.0 ** -SOLVED_OCTAVES
            for c in range(2):
                out[f, s, c] = decode(r4[f, s, c], low, SOLVED_OCTAVES)

    def mixed(f, start, stop, g):
        per = np_ // (stop - start)

        @pl.loop(start, stop)
        def _(i):
            @pl.when(i > 0)
            def _():
                send_z(f, i)

            for j in range(per):
                k = (i - start) * per + j

                @pl.when(k > 0)
                def _():
                    send_xy(g, k)

    transform(0)
    pl.loop(1, nz_)(functools.partial(send_z, 0))
    transform(1)
    pl.loop(1, nz_)(functools.partial(send_z, 1))
    transform(2)
    regroup(0)
    mixed(2, 0, nz_ // 2, 0)
    regroup(1)
    mixed(2, nz_ // 2, nz_, 1)
    solve(0)
    pl.loop(0, YS // 2)(functools.partial(send_far, 0))
    regroup(2)

    @pl.loop(YS // 2, YS)
    def _(y):
        send_far(0, y)
        per = np_ // (YS - YS // 2)
        for j in range(per):
            k = (y - YS // 2) * per + j

            @pl.when(k > 0)
            def _():
                send_xy(2, k)

    send_near(0)
    solve(1)
    pl.loop(0, YS)(functools.partial(send_far, 1))
    send_near(1)
    relay(0)
    solve(2)
    pl.loop(0, YS)(functools.partial(send_far, 2))
    send_near(2)
    relay(1)
    unpack(0)
    relay(2)
    unpack(1)
    unpack(2)

    drain(mx1r.at[pl.ds(0, nm - 1)], mx_s.at[0])
    drain(mx2r.at[pl.ds(0, nrad - 1)], mx_s.at[1])
    for f in range(fields):
        drain(r1.at[f, pl.ds(0, nm - 1)], t1_s.at[f])
        drain(r2.at[f, pl.ds(0, nz_ - 1)], z_s.at[f])
        drain(r3.at[f, pl.ds(0, np_ - 1)], xy_s.at[f])
        drain(scr.at[f, pl.ds(0, nrad - 1)], sc_s.at[f])
        drain(r4.at[f, pl.ds(0, YS - 1)], t4_s.at[f])
        drain(r4.at[f, pl.ds(0, YS)], rp_s.at[f])
        drain(r4.at[f, pl.ds(0, YS)], fw_s.at[f])


def per_device(forcing, diffusion, axial_forward, axial_inverse_map, axial_eigenvalues,
               radial_forward, radial_backward, radial_eigenvalues):
    fields, slab, rblock, nz = forcing.shape
    nm, nrad = lax.axis_size("modes"), lax.axis_size("rad")
    points, cols = slab * nm, nz // CORES
    nzs, nps = Z_HI * Z_LO, YS * XS * CORES
    tables = [jnp.asarray(t) for t in small_tables(points)]
    dma = pltpu.SemaphoreType.DMA
    vmem = pl.BlockSpec(memory_space=pltpu.VMEM)
    args = (forcing, *tables, diffusion.reshape(1, fields), axial_forward, axial_inverse_map, axial_eigenvalues.reshape(1, nz),
            radial_forward, radial_backward, radial_eigenvalues)
    args = [pltpu.with_memory_space_constraint(a, pltpu.HBM) for a in args]
    specs = [pl.BlockSpec(memory_space=pltpu.HBM)] * len(args)
    return pl.pallas_call(
        kernel,
        out_shape=jax.ShapeDtypeStruct((fields, nrad, 2, rblock, nz), F32),
        in_specs=specs,
        out_specs=vmem,
        scratch_shapes=[
            pltpu.VMEM((2 * nzs * nps, points), BF16), pltpu.VMEM((2 * nzs * nps, points), BF16),
            pltpu.VMEM((fields, nm, slab, cols), BF16),
            pltpu.VMEM((fields, nzs, 2 * nps, cols), BF16), pltpu.VMEM((fields, nzs, 2 * nps, cols), BF16),
            pltpu.VMEM((nzs * 2 * nps, cols), F32),
            pltpu.VMEM((fields, nps, 2 * nzs, cols), BF16), pltpu.VMEM((fields, nps, 2 * nzs, cols), BF16),
            pltpu.VMEM((2, rblock * nrad, nz), F32),
            pltpu.VMEM((fields, nrad, 2, rblock, nz), BF16), pltpu.VMEM((fields, nrad, 2, rblock, nz), BF16),
            pltpu.VMEM((1, cols), F32), pltpu.VMEM((nm, 1, cols), F32),
            pltpu.VMEM((1, cols), F32), pltpu.VMEM((nrad, 1, cols), F32),
            pltpu.VMEM((fields, 1, nz), F32), pltpu.VMEM((fields, nrad, 1, nz), F32),
            dma((fields,)), dma((fields,)), dma((2,)), dma((2,)), dma((fields,)), dma((fields,)),
            dma((fields,)), dma((fields,)), dma((fields,)), dma((fields,)), dma((fields,)), dma((fields,)),
            pltpu.VMEM((fields, 2, YS, rblock, nz), BF16), dma((fields,)), dma((fields, 2)), dma((fields,)),
            pltpu.VMEM((rblock * nrad, nz), F32), pltpu.VMEM((fields, nm, slab, cols), BF16),
            pltpu.VMEM((CORES, slab * rblock, cols), F32),
            *(pltpu.VMEM(a.shape, a.dtype) for a in args), dma((len(args),)),
        ],
        compiler_params=pltpu.CompilerParams(collective_id=0, has_side_effects=True, vmem_limit_bytes=48 << 20),
    )(*args)


def solution(mesh):
    in_specs = (P(None, "modes", "rad", None), P(), P(), P(), P(),
                P(("modes", "rad"), None, None), P(("modes", "rad"), None, None),
                P(("modes", "rad"), None))
    return jax.shard_map(per_device, mesh=mesh, in_specs=in_specs,
                         out_specs=P(None, "modes", None, "rad", None), check_vma=False)
```

```python
import functools
import math

import jax
import jax.numpy as jnp
import numpy as np
from jax import lax
from jax.experimental import pallas as pl
from jax.experimental.pallas import tpu as pltpu
from jax.sharding import PartitionSpec as P

F32, BF16 = jnp.float32, jnp.bfloat16
MESH = pl.DeviceIdType.MESH
Z_LO, XS, CORES, Z_HI, YS = 8, 4, 2, 2, 4
SPECTRUM_OCTAVES, SOLVED_OCTAVES = 16, 10
TINY = 1e-30


def encode(x, inverse_floor, octaves):
    grown = jnp.log2(1.0 + jnp.abs(x) * inverse_floor)
    code = jnp.exp2(grown * (239.0 / octaves) - 120.0)
    return jnp.where(x < 0, -code, code).astype(BF16)


def decode(code, floor, octaves):
    code = code.astype(F32)
    grown = (jnp.log2(jnp.abs(code)) + 120.0) * (octaves / 239.0)
    size = (jnp.exp2(grown) - 1.0) * floor
    return jnp.where(code < 0, -size, size)


def split(x):
    high = x.astype(BF16)
    return high, (x - high.astype(F32)).astype(BF16)


def dot3(a, b, dims):
    d = functools.partial(lax.dot_general, dimension_numbers=(dims, ((), ())), preferred_element_type=F32)
    return d(a[0], b[0]) + (d(a[0], b[1]) + d(a[1], b[0]))


NN, NT_ = ((1,), (0,)), ((1,), (1,))


def mode_of(z, p):
    m = (z % Z_LO) * (XS * CORES) + p % (XS * CORES)
    return m * (Z_HI * YS) + (z // Z_LO) * YS + p // (XS * CORES)


def small_tables(points):
    k = [mode_of(z, 0) for z in range(Z_HI * Z_LO)] + [mode_of(0, p) for p in range(YS * XS * CORES)]
    turns = np.outer(np.array(k), np.arange(points)) % points
    radians = turns * (2.0 * math.pi / points)
    return np.cos(radians).astype(np.float32), np.sin(radians).astype(np.float32)


def kernel(forcing_, cosine_, sine_, diff_, af_, ai_, qeig_, rf_, rb_, reig_, out,
           up, lo, r1, enc, r2, flat, s3, r3, x, s4, r4, mx1, mx1r, mx2, mx2r, sc, scr,
           t1_s, t1_r, mx_s, mx_r, z_s, z_r, xy_s, xy_r, t4_s, t4_r, sc_s, sc_r, rp, rp_s, rp_r, fw_s, fw_r, eigen, xs, wide,
           forcing, cosine, sine, diff, af, ai, qeig, rf, rb, reig, in_s):
    me, rad = lax.axis_index("modes"), lax.axis_index("rad")
    fields, nm, slab, cols = xs.shape
    nrad, nz_, np_ = Z_HI * YS, Z_HI * Z_LO, YS * XS * CORES
    points = nm * slab
    rblock = XS * Z_LO
    nr, nz = rblock * nrad, CORES * cols
    inner = XS * CORES
    z, p = (rad // YS) * Z_LO + me // inner, (rad % YS) * inner + me % inner

    def at(zz, pp):
        return ((zz % Z_LO) * inner + pp % inner, (zz // Z_LO) * YS + pp // inner)

    def send(src, dst, s, r, to):
        pltpu.make_async_remote_copy(src_ref=src, dst_ref=dst, send_sem=s, recv_sem=r, device_id=to,
                                     device_id_type=MESH).start()

    def drain(ref, sem):
        pltpu.make_async_copy(ref, ref, sem).wait()

    loads = [pltpu.make_async_copy(forcing_, forcing, in_s.at[0])]
    for n, (src, dst) in enumerate(((cosine_, cosine), (sine_, sine), (diff_, diff), (af_, af), (ai_, ai), (qeig_, qeig), (rf_, rf),
                                  (rb_, rb), (reig_, reig))):
        loads.append(pltpu.make_async_copy(src, dst, in_s.at[n + 1]))
    loads[0].start()
    barrier = pltpu.get_barrier_semaphore()

    @pl.loop(1, nm)
    def _(i):
        pl.semaphore_signal(barrier, inc=1, device_id=((me + i) % nm, rad), device_id_type=MESH)

    @pl.loop(1, nrad)
    def _(i):
        pl.semaphore_signal(barrier, inc=1, device_id=(me, (rad + i) % nrad), device_id_type=MESH)

    def spread(f):
        for core in range(CORES):
            wide[core] = forcing[f, :, :, core * cols:(core + 1) * cols].astype(F32).reshape(slab * rblock, cols)
        for m in range(nm):
            row = m // CORES % XS * Z_LO + m // inner
            xs[f, m] = wide[m % CORES, pl.ds(row, slab, stride=rblock), :].astype(BF16)

    def begin(f):
        @pl.loop(1, nm)
        def _(i):
            m = (me + i) % nm
            send(xs.at[f, m], r1.at[f, me], t1_s.at[f], t1_r.at[f], (m, rad))

    for load in loads[1:]:
        load.start()
    loads[0].wait()
    spread(0)
    pl.semaphore_wait(barrier, nm + nrad - 2)
    begin(0)
    top = jnp.zeros((slab, cols), F32)
    for f in range(fields):
        for core in range(CORES):
            top = jnp.maximum(top, jnp.max(
                jnp.abs(forcing[f, :, :, core * cols:(core + 1) * cols].astype(F32)), axis=1))
    top = jnp.max(jnp.max(top, axis=0, keepdims=True), axis=1, keepdims=True)
    mx1[...] = jnp.broadcast_to(top, (1, cols))

    @pl.loop(1, nm)
    def _(i):
        send(mx1, mx1r.at[me], mx_s.at[0], mx_r.at[0], ((me + i) % nm, rad))

    mx1r[me] = mx1[...]
    spread(1)
    begin(1)
    spread(2)
    drain(mx1r.at[pl.ds(0, nm - 1)], mx_r.at[0])
    top = jnp.max(mx1r[...], axis=0)
    mx2[...] = top
    mx2r[rad] = top

    @pl.loop(1, nrad)
    def _(i):
        send(mx2, mx2r.at[rad], mx_s.at[1], mx_r.at[1], (me, (rad + i) % nrad))

    begin(2)
    for f in range(fields):
        r1[f, me] = xs[f, me]

    for load in loads[1:]:
        load.wait()
    half, hop, scale = 2 * np_, nz_ // 4, 1.0 / math.sqrt(points)
    eigen[...] = jnp.transpose(jnp.broadcast_to(reig[...], (nz, nr))) + qeig[...]

    @pl.loop(0, nz_)
    def _(a):
        ca, sa = cosine[pl.ds(a, 1), :] * scale, sine[pl.ds(a, 1), :] * scale
        cb, sb = cosine[nz_:, :], sine[nz_:, :]
        for c, table in enumerate((ca * cb - sa * sb, -(sa * cb + ca * sb))):
            high, low = split(table)
            rows = pl.ds(pl.multiple_of(a * half + c * np_, np_), np_)
            up[rows, :] = high
            lo[rows, :] = low

    drain(mx2r.at[pl.ds(0, nrad - 1)], mx_r.at[1])
    bound = jnp.maximum(jnp.max(mx2r[...], axis=0), TINY)
    floor = bound * 2.0 ** (5 - SPECTRUM_OCTAVES)
    inverse_floor = 2.0 ** (SPECTRUM_OCTAVES - 5) / bound
    blocks = 4
    each = nz_ // blocks

    def transform(f):
        drain(r1.at[f, pl.ds(0, nm - 1)], t1_r.at[f])
        data = r1[f].reshape(points, cols)

        @pl.loop(0, blocks)
        def _(b):
            rows = pl.ds(pl.multiple_of(b * each * half, each * half), each * half)
            spec = jnp.dot(up[rows, :], data, preferred_element_type=F32) + jnp.dot(
                lo[rows, :], data, preferred_element_type=F32)
            enc[f, pl.ds(b * each, each)] = encode(spec, inverse_floor, SPECTRUM_OCTAVES).reshape(each, half, cols)
        r2[f, z] = enc[f, z]

    def send_z(f, i):
        to = (z + i) % nz_
        send(enc.at[f, to], r2.at[f, z], z_s.at[f], z_r.at[f], at(to, p))

    def regroup(f):
        drain(r2.at[f, pl.ds(0, nz_ - 1)], z_r.at[f])
        flat[...] = r2[f].astype(F32).reshape(nz_ * half, cols)
        for q in range(np_):
            for c in range(2):
                s3[f, q, c * nz_:(c + 1) * nz_, :] = flat[pl.ds(c * np_ + q, nz_, stride=half), :].astype(BF16)
        r3[f, p] = s3[f, p]

    def send_xy(f, i):
        to = (p + i) % np_
        send(s3.at[f, to], r3.at[f, p], xy_s.at[f], xy_r.at[f], at(z, to))

    def solve(f):
        drain(r3.at[f, pl.ds(0, np_ - 1)], xy_r.at[f])
        for q in range(np_):
            y, xx, core = q // inner, (q // CORES) % XS, q % CORES
            value = decode(r3[f, q], floor, SPECTRUM_OCTAVES)
            for c in range(2):
                for h in range(Z_HI):
                    r0 = (h * YS + y) * rblock + xx * Z_LO
                    x[c, r0:r0 + Z_LO, core * cols:(core + 1) * cols] = value[
                        c * nz_ + h * Z_LO:c * nz_ + (h + 1) * Z_LO]
        axial = dot3(split(x[...].reshape(2 * nr, nz)), split(af[...]), NT_)
        denominator = 1.0 + diff[0:1, f:f + 1] * eigen[...]
        result = []
        for c in range(2):
            scaled = dot3(split(rf[0]), split(axial[c * nr:(c + 1) * nr]), NN) / denominator
            result.append(dot3(split(dot3(split(rb[0]), split(scaled), NN)), split(ai[...]), NT_))
        top = jnp.maximum(jnp.max(jnp.abs(result[0]), axis=0, keepdims=True),
                          jnp.max(jnp.abs(result[1]), axis=0, keepdims=True))
        top = jnp.maximum(jnp.broadcast_to(jnp.max(top, axis=1, keepdims=True), (1, nz)), TINY)
        sc[f] = top
        scr[f, rad] = top
        inverse = 2.0 ** SOLVED_OCTAVES / top
        for c in range(2):
            code = encode(result[c], inverse, SOLVED_OCTAVES)
            for s in range(nrad):
                s4[f, s, c] = code[s * rblock:(s + 1) * rblock]

        r4[f, rad] = s4[f, rad]

    far = (1 - rad // YS) * YS

    def send_far(f, y):
        send(s4.at[f, far + y, 0], rp.at[f, 0, rad % YS], rp_s.at[f], rp_r.at[f, 0],
             at((z + hop) % nz_, y * inner + p % inner))
        send(s4.at[f, far + y, 1], rp.at[f, 1, rad % YS], rp_s.at[f], rp_r.at[f, 1],
             at((z + nz_ - hop) % nz_, y * inner + p % inner))

    def send_near(f):
        @pl.loop(1, nrad)
        def _(i):
            send(sc.at[f], scr.at[f, rad], sc_s.at[f], sc_r.at[f], (me, (rad + i) % nrad))

        @pl.loop(1, YS)
        def _(i):
            to = rad // YS * YS + (rad + i) % YS
            send(s4.at[f, to], r4.at[f, rad], t4_s.at[f], t4_r.at[f], (me, to))

    def relay(f):
        for part, step in ((0, hop), (1, nz_ - hop)):
            drain(rp.at[f, part], rp_r.at[f, part])
            source = (z + nz_ - step) % nz_ // Z_LO * YS
            send(rp.at[f, part], r4.at[f, pl.ds(source, YS), part], fw_s.at[f], fw_r.at[f], at((z + step) % nz_, p))

    def unpack(f):
        drain(scr.at[f, pl.ds(0, nrad - 1)], sc_r.at[f])

        def widen(s):
            low = scr[f, s] * 2.0 ** -SOLVED_OCTAVES
            for c in range(2):
                out[f, s, c] = decode(r4[f, s, c], low, SOLVED_OCTAVES)

        drain(r4.at[f, pl.ds(0, YS - 1)], t4_r.at[f])
        pl.loop(rad // YS * YS, rad // YS * YS + YS)(widen)
        drain(r4.at[f, pl.ds(0, YS)], fw_r.at[f])
        pl.loop(far, far + YS)(widen)

    def mixed(f, start, stop, g):
        per = np_ // (stop - start)

        @pl.loop(start, stop)
        def _(i):
            @pl.when(i > 0)
            def _():
                send_z(f, i)

            for j in range(per):
                k = (i - start) * per + j

                @pl.when(k > 0)
                def _():
                    send_xy(g, k)

    transform(0)
    pl.loop(1, nz_)(functools.partial(send_z, 0))
    transform(1)
    pl.loop(1, nz_)(functools.partial(send_z, 1))
    transform(2)
    regroup(0)
    mixed(2, 0, nz_ // 2, 0)
    regroup(1)
    mixed(2, nz_ // 2, nz_, 1)
    solve(0)
    pl.loop(0, YS // 2)(functools.partial(send_far, 0))
    regroup(2)

    @pl.loop(YS // 2, YS)
    def _(y):
        send_far(0, y)
        per = np_ // (YS - YS // 2)
        for j in range(per):
            k = (y - YS // 2) * per + j

            @pl.when(k > 0)
            def _():
                send_xy(2, k)

    send_near(0)
    solve(1)
    pl.loop(0, YS)(functools.partial(send_far, 1))
    send_near(1)
    relay(0)
    solve(2)
    pl.loop(0, YS)(functools.partial(send_far, 2))
    send_near(2)
    relay(1)
    unpack(0)
    relay(2)
    unpack(1)
    unpack(2)

    drain(mx1r.at[pl.ds(0, nm - 1)], mx_s.at[0])
    drain(mx2r.at[pl.ds(0, nrad - 1)], mx_s.at[1])
    for f in range(fields):
        drain(r1.at[f, pl.ds(0, nm - 1)], t1_s.at[f])
        drain(r2.at[f, pl.ds(0, nz_ - 1)], z_s.at[f])
        drain(r3.at[f, pl.ds(0, np_ - 1)], xy_s.at[f])
        drain(scr.at[f, pl.ds(0, nrad - 1)], sc_s.at[f])
        drain(r4.at[f, pl.ds(0, YS - 1)], t4_s.at[f])
        drain(r4.at[f, pl.ds(0, YS)], rp_s.at[f])
        drain(r4.at[f, pl.ds(0, YS)], fw_s.at[f])


def per_device(forcing, diffusion, axial_forward, axial_inverse_map, axial_eigenvalues,
               radial_forward, radial_backward, radial_eigenvalues):
    fields, slab, rblock, nz = forcing.shape
    nm, nrad = lax.axis_size("modes"), lax.axis_size("rad")
    points, cols = slab * nm, nz // CORES
    nzs, nps = Z_HI * Z_LO, YS * XS * CORES
    tables = [jnp.asarray(t) for t in small_tables(points)]
    dma = pltpu.SemaphoreType.DMA
    vmem = pl.BlockSpec(memory_space=pltpu.VMEM)
    args = (forcing, *tables, diffusion.reshape(1, fields), axial_forward, axial_inverse_map, axial_eigenvalues.reshape(1, nz),
            radial_forward, radial_backward, radial_eigenvalues)
    args = [pltpu.with_memory_space_constraint(a, pltpu.HBM) for a in args]
    specs = [pl.BlockSpec(memory_space=pltpu.HBM)] * len(args)
    return pl.pallas_call(
        kernel,
        out_shape=jax.ShapeDtypeStruct((fields, nrad, 2, rblock, nz), F32),
        in_specs=specs,
        out_specs=vmem,
        scratch_shapes=[
            pltpu.VMEM((2 * nzs * nps, points), BF16), pltpu.VMEM((2 * nzs * nps, points), BF16),
            pltpu.VMEM((fields, nm, slab, cols), BF16),
            pltpu.VMEM((fields, nzs, 2 * nps, cols), BF16), pltpu.VMEM((fields, nzs, 2 * nps, cols), BF16),
            pltpu.VMEM((nzs * 2 * nps, cols), F32),
            pltpu.VMEM((fields, nps, 2 * nzs, cols), BF16), pltpu.VMEM((fields, nps, 2 * nzs, cols), BF16),
            pltpu.VMEM((2, rblock * nrad, nz), F32),
            pltpu.VMEM((fields, nrad, 2, rblock, nz), BF16), pltpu.VMEM((fields, nrad, 2, rblock, nz), BF16),
            pltpu.VMEM((1, cols), F32), pltpu.VMEM((nm, 1, cols), F32),
            pltpu.VMEM((1, cols), F32), pltpu.VMEM((nrad, 1, cols), F32),
            pltpu.VMEM((fields, 1, nz), F32), pltpu.VMEM((fields, nrad, 1, nz), F32),
            dma((fields,)), dma((fields,)), dma((2,)), dma((2,)), dma((fields,)), dma((fields,)),
            dma((fields,)), dma((fields,)), dma((fields,)), dma((fields,)), dma((fields,)), dma((fields,)),
            pltpu.VMEM((fields, 2, YS, rblock, nz), BF16), dma((fields,)), dma((fields, 2)), dma((fields,)), dma((fields,)),
            pltpu.VMEM((rblock * nrad, nz), F32), pltpu.VMEM((fields, nm, slab, cols), BF16),
            pltpu.VMEM((CORES, slab * rblock, cols), F32),
            *(pltpu.VMEM(a.shape, a.dtype) for a in args), dma((len(args),)),
        ],
        compiler_params=pltpu.CompilerParams(collective_id=0, has_side_effects=True, vmem_limit_bytes=48 << 20),
    )(*args)


def solution(mesh):
    in_specs = (P(None, "modes", "rad", None), P(), P(), P(), P(),
                P(("modes", "rad"), None, None), P(("modes", "rad"), None, None),
                P(("modes", "rad"), None))
    return jax.shard_map(per_device, mesh=mesh, in_specs=in_specs,
                         out_specs=P(None, "modes", None, "rad", None), check_vma=False)
```
